1024 devices in a mesh: ctx: 128 (over x, z, core), tp: 8 (over y).
Axes of the slice: x: 4, y: 8, z: 16, core: 2. Of those that a mesh axis runs over, the one named last changes fastest.
Arguments:
- streams: bfloat16 [3, 16384, 8192], P(None, 'ctx', 'tp'), may hold values from -6 to 6
- short_filter: bfloat16 [3, 512, 7], P(None, 'tp'), may hold values from -3 to 3
- decay_rate: float32 [16, 8192], P(None, 'tp'), may hold values from 1.8310548e-05 to 0.05
- residue: float32 [16, 8192], P(None, 'tp'), may hold values from -5 to 5
- norm_gain: float32 [8192], P('tp'), may hold values from 0.5 to 1.5
- out_grad: bfloat16 [16384, 8192], P('ctx', 'tp'), may hold values from -6 to 6
Outputs:
- output: bfloat16 [16384, 8192], P('ctx', 'tp')
- stream_grads: bfloat16 [3, 16384, 8192], P(None, 'ctx', 'tp')
The draws below stay inside these ranges and needn't reach their ends.
All inputs are finite; a program needn't handle non-finite values.
Results may differ from the reference program's by a relative error of at most 0.002.
Values may be sent and summed in bfloat16 or wider, within the bound.
A program may use at most 64 MiB of HBM per device.

```python
import math
import jax
import jax.numpy as jnp
from jax import lax

D = 8192
MODES = 16
TAPS = 7
GROUP = 16
BLOCK = 16
SEQ = 16384


def level_of(own_key, shape, split, smallest, high):
    loudness = 1.0
    for position, blocks in split:
        draws = jax.random.uniform(jax.random.fold_in(jax.random.fold_in(own_key, 6), position), (blocks,), jnp.float32, smallest / len(split), high / len(split))
        loudness = loudness * jnp.repeat(jnp.exp(draws), shape[position] // blocks).reshape((-1,) + (1,) * (len(shape) - 1 - position))
    return loudness


def gaussian(own_key, dims, width, bound, shards=(), held_as=jnp.bfloat16):
    drawn = jax.random.normal(own_key, dims, jnp.float32) * width
    if len(shards) > 0:
        drawn = level_of(own_key, dims, shards, -0.22, 0.18) * drawn
    return jnp.clip(drawn, min=-bound, max=bound).astype(held_as)


def setup_inputs(seed: int = 0) -> dict:
    seeds = jax.random.split(jax.random.key(seed), 7)
    streams = gaussian(seeds[0], (3, SEQ, D), 1.0, 6.0, ((1, 128), (2, 8)))
    short_filter = gaussian(seeds[1], (3, D // GROUP, TAPS), 0.5, 3.0, ((1, 8),))
    decay_rate = jnp.clip(jnp.exp(math.log(0.05) - 7.912301 * jax.random.uniform(seeds[2], (MODES, D), jnp.float32) ** level_of(seeds[2], (MODES, D), ((1, 8),), -0.2, 0.2)), 1.831054760259576e-05, 0.05)
    residue = gaussian(seeds[3], (MODES, D), 1.0, 5.0, ((1, 8),), jnp.float32)
    norm_gain = jnp.clip(1.0 + 0.1 * jax.random.normal(seeds[4], (D,), jnp.float32), 0.5, 1.5)
    out_grad = gaussian(seeds[5], (SEQ, D), 1.0, 6.0, ((0, 128), (1, 8)))
    return {"streams": streams, "short_filter": short_filter, "decay_rate": decay_rate, "residue": residue, "norm_gain": norm_gain, "out_grad": out_grad}


EPSILON = 1e-05

def channel_weights(short_filter):
    stream_count, group_count, tap_count = short_filter.shape
    spread = jnp.broadcast_to(short_filter.astype(jnp.float32)[:, :, None, :], (stream_count, group_count, GROUP, tap_count))
    return jnp.transpose(spread.reshape(stream_count, group_count * GROUP, tap_count), (0, 2, 1))

def filter_tables(decay_rate, residue):
    lag_steps = jnp.arange(BLOCK, dtype=jnp.float32)
    scaled = residue * jnp.sqrt(2.0 * decay_rate)
    places = jnp.arange(BLOCK, dtype=jnp.int32)
    lagged = places[:, None] - places[None, :]
    lag_float = jnp.maximum(lagged, 0).astype(jnp.float32)
    terms = scaled[:, None, None, :] * jnp.exp(-decay_rate[:, None, None, :] * lag_float[None, :, :, None])
    toeplitz = jnp.where((lagged >= 0)[:, :, None], lax.optimization_barrier(jnp.sum(terms, axis=0)), jnp.zeros((), jnp.float32))
    end_weight = jnp.exp(-decay_rate[:, None, :] * (BLOCK - 1.0 - lag_steps)[None, :, None])
    out_weight = scaled[:, None, :] * jnp.exp(-decay_rate[:, None, :] * (lag_steps + 1.0)[None, :, None])
    return (toeplitz, end_weight, out_weight)

def causal_modal(signal, tables, block_decay):
    toeplitz, end_weight, out_weight = tables
    pieces = signal.reshape(-1, BLOCK, signal.shape[-1])

    def advance(carried_state, block_rows):
        within = lax.optimization_barrier(jnp.sum(toeplitz * block_rows[None, :, :], axis=1))
        carried = lax.optimization_barrier(jnp.sum(out_weight * carried_state[:, None, :], axis=0))
        ending = lax.optimization_barrier(jnp.sum(end_weight * block_rows[None, :, :], axis=1))
        return (block_decay * carried_state + ending, within + carried)
    zero_state = jnp.zeros(block_decay.shape, jnp.float32)
    return lax.scan(advance, zero_state, pieces)[1].reshape(signal.shape)

def short_causal(signal, weights):
    reach_rows = weights.shape[1] - 1
    length = signal.shape[1]
    padded = jnp.pad(signal, ((0, 0), (reach_rows, 0), (0, 0)))
    summed = weights[:, 0, None, :] * signal
    for offset in range(1, reach_rows + 1):
        summed = summed + weights[:, offset, None, :] * padded[:, reach_rows - offset:reach_rows - offset + length, :]
    return summed

def short_anticausal(signal, weights):
    reach_rows = weights.shape[1] - 1
    length = signal.shape[1]
    padded = jnp.pad(signal, ((0, 0), (0, reach_rows), (0, 0)))
    summed = weights[:, 0, None, :] * signal
    for offset in range(1, reach_rows + 1):
        summed = summed + weights[:, offset, None, :] * padded[:, offset:offset + length, :]
    return summed

def reference(streams, short_filter, decay_rate, residue, norm_gain, out_grad):
    stream_count, length, full_width = streams.shape
    piece_width = math.gcd(full_width, 1024)
    piece_count = full_width // piece_width
    weights_all = channel_weights(short_filter)

    def forward(piece_index):
        first_column = piece_index * piece_width
        stream_part = lax.dynamic_slice_in_dim(streams, first_column, piece_width, 2)
        weights = lax.dynamic_slice_in_dim(weights_all, first_column, piece_width, 2)
        rate_part = lax.dynamic_slice_in_dim(decay_rate, first_column, piece_width, 1)
        residue_part = lax.dynamic_slice_in_dim(residue, first_column, piece_width, 1)
        gain_part = lax.dynamic_slice_in_dim(norm_gain, first_column, piece_width, 0)
        grad_part = lax.dynamic_slice_in_dim(out_grad, first_column, piece_width, 1)
        convolved = short_causal(stream_part.astype(jnp.float32), weights)
        tables = filter_tables(rate_part, residue_part)
        block_decay = jnp.exp(-rate_part * BLOCK)
        long_conv = causal_modal(convolved[1] * convolved[2], tables, block_decay)
        modulated = convolved[0] * long_conv
        scaled_grad = gain_part * grad_part.astype(jnp.float32)
        return (convolved, tables, block_decay, long_conv, modulated, scaled_grad, weights, gain_part)

    def statistics(piece_index):
        parts = forward(piece_index)
        modulated, scaled_grad = (parts[4], parts[5])
        return (lax.optimization_barrier(jnp.sum(modulated * modulated, axis=1)), lax.optimization_barrier(jnp.sum(scaled_grad * modulated, axis=1)))
    indices = jnp.arange(piece_count, dtype=jnp.int32)
    squares, crosses = lax.map(statistics, indices)
    inverse = lax.rsqrt(lax.optimization_barrier(jnp.sum(squares, axis=0)) / full_width + EPSILON)
    cross_mean = lax.optimization_barrier(jnp.sum(crosses, axis=0)) / full_width

    def finish(piece_index):
        convolved, tables, block_decay, long_conv, modulated, scaled_grad, weights, gain_part = forward(piece_index)
        output = (gain_part * modulated * inverse[:, None]).astype(jnp.bfloat16)
        mixed_grad = inverse[:, None] * scaled_grad - modulated * (inverse * inverse * inverse * cross_mean)[:, None]
        query_grad = mixed_grad * long_conv
        long_grad = mixed_grad * convolved[0]
        gated_grad = jnp.flip(causal_modal(jnp.flip(long_grad, axis=0), tables, block_decay), axis=0)
        conv_grad = jnp.stack([query_grad, gated_grad * convolved[2], gated_grad * convolved[1]])
        return (output, short_anticausal(conv_grad, weights).astype(jnp.bfloat16))
    outputs, grads = lax.map(finish, indices)
    output = jnp.transpose(outputs, (1, 0, 2)).reshape(length, full_width)
    stream_grads = jnp.transpose(grads, (1, 2, 0, 3)).reshape(stream_count, length, full_width)
    return (output, stream_grads)
```

```python
import functools

import jax
import jax.numpy as jnp
from jax import lax
from jax.experimental import pallas as pl
from jax.experimental.pallas import tpu as pltpu
from jax.sharding import PartitionSpec as P

MESH = pl.DeviceIdType.MESH
F32 = jnp.float32
BF16 = jnp.bfloat16
GROUP = 16
EPSILON = 1e-05
ROWS = 128
EXT = 8
HALO = 8
TAPS = 7
MODES = 16
SUB = 8
LANES = 128
TILES = 8
ROW_DEVICES = 32
X_COUNT = 4
BLOCKS = (ROWS + EXT) // 8


def rows_of(ref, start, count):
    offset = start * SUB
    if not isinstance(offset, int):
        offset = pl.multiple_of(offset, SUB)
    return ref[pl.ds(offset, count * SUB), :].reshape(count, SUB, LANES)


def put_rows(ref, start, value):
    offset = start * SUB
    if not isinstance(offset, int):
        offset = pl.multiple_of(offset, SUB)
    ref[pl.ds(offset, value.shape[0] * SUB), :] = value.reshape(value.shape[0] * SUB, LANES)


def spread(ref, start, tile, value):
    ref[pl.ds(start * SUB + tile, value.shape[0], stride=SUB), :] = value


def gathered(ref, start, count, tile):
    return ref[pl.ds(start * SUB + tile, count, stride=SUB), :]


def kernel(
    streams_hbm, filter_ref, rate_ref, residue_ref, gain_ref, grad_hbm,
    output_hbm, grads_hbm,
    xin, gin, obuf, gbuf, s_ref, w_ref, r_ref, sc_ref, rt_ref, q_ref, k_ref, v_ref, u_ref, og_ref, sg_ref, y_ref, m_ref,
    lg_ref, qg_ref, part_ref, inv_ref, cw_ref, rate4, pow_ref,
    ebuf_f, erecv_f, pbuf_f, irecv_f, rbuf_f, rrecv_f,
    ebuf_b, erecv_b, pbuf_b, irecv_b, rbuf_b, rrecv_b,
    sums, sums_recv,
    in_sem, out_sem, halo_send, halo_recv, up_send, up_recv, down_send, down_recv, x_send, x_recv, y_send, y_recv,
):
    ctx = lax.axis_index("ctx")
    tp = lax.axis_index("tp")
    place = lax.rem(ctx, ROW_DEVICES)
    row = lax.div(ctx, ROW_DEVICES)
    ctx_count = ROW_DEVICES * X_COUNT
    next_ctx = lax.rem(ctx + 1, ctx_count)
    prev_ctx = lax.rem(ctx + ctx_count - 1, ctx_count)

    load_x = pltpu.make_async_copy(streams_hbm, xin, in_sem.at[0])
    load_g = pltpu.make_async_copy(grad_hbm, gin, in_sem.at[1])
    load_x.start()
    load_g.start()

    barrier = pltpu.get_barrier_semaphore()

    def greet_ctx(peer):
        pl.semaphore_signal(barrier, inc=1, device_id={"ctx": peer}, device_id_type=MESH)

    greet_ctx(next_ctx)
    greet_ctx(prev_ctx)

    @pl.loop(1, ROW_DEVICES)
    def _(i):
        greet_ctx(row * ROW_DEVICES + lax.rem(place + i, ROW_DEVICES))

    @pl.loop(1, X_COUNT)
    def _(i):
        greet_ctx(lax.rem(row + i, X_COUNT) * ROW_DEVICES + place)

    @pl.loop(1, 8)
    def _(i):
        pl.semaphore_signal(barrier, inc=1, device_id={"tp": lax.rem(tp + i, 8)}, device_id_type=MESH)

    for half in range(2):
        for tile in range(TILES):
            lanes = slice(tile * LANES, (tile + 1) * LANES)
            rate = rate_ref[half * 8 : half * 8 + 8, lanes]
            residue = residue_ref[half * 8 : half * 8 + 8, lanes]
            spread(rt_ref, half * 8, tile, rate)
            spread(r_ref, half * 8, tile, jnp.exp(-rate))
            spread(sc_ref, half * 8, tile, residue * jnp.sqrt(2.0 * rate))
    groups = filter_ref.shape[2]
    spreader = (
        lax.broadcasted_iota(jnp.int32, (groups, TILES * LANES), 1) // GROUP
        == lax.broadcasted_iota(jnp.int32, (groups, TILES * LANES), 0)
    ).astype(F32)
    for s in range(3):
        taps = lax.dot_general(
            filter_ref[s].astype(F32), spreader, (((1,), (0,)), ((), ())), precision=lax.Precision.HIGHEST,
            preferred_element_type=F32,
        )
        for tile in range(TILES):
            spread(w_ref.at[s], 0, tile, taps[:, tile * LANES : (tile + 1) * LANES])
    for mode in range(MODES):
        rates = rt_ref[mode * SUB : mode * SUB + SUB, :]
        rate4[2 * mode] = rates[0:4]
        rate4[2 * mode + 1] = rates[4:8]
    own_rate = rate4[place] * float(ROWS)

    @pl.loop(0, ROW_DEVICES + 1)
    def _(i):
        pow_ref[i] = jnp.exp(-own_rate * i.astype(F32))

    decay = rows_of(r_ref, 0, MODES)

    load_x.wait()

    @pl.loop(0, ROWS // 16)
    def _(b):
        for s in range(3):
            for tile in range(TILES):
                value = xin[s, pl.ds(b * 16, 16), tile * LANES : (tile + 1) * LANES].astype(F32)
                spread(s_ref.at[s], HALO + b * 16, tile, value)

    load_g.wait()
    gain = gain_ref[...]

    @pl.loop(0, ROWS // 16)
    def _(b):
        for tile in range(TILES):
            value = gin[pl.ds(b * 16, 16), tile * LANES : (tile + 1) * LANES].astype(F32)
            spread(og_ref, b * 16, tile, value)

    def short(target, s, start):
        window = rows_of(s_ref.at[s], start + HALO - (TAPS - 1), 8 + TAPS - 1)
        total = rows_of(w_ref.at[s], 0, 1) * window[TAPS - 1 : TAPS - 1 + 8]
        for tap in range(1, TAPS):
            total = total + rows_of(w_ref.at[s], tap, 1) * window[TAPS - 1 - tap : TAPS - 1 - tap + 8]
        if target is not None:
            put_rows(target, start, total)
        return total

    def gated(start):
        keys = short(k_ref, 1, start)
        values = short(v_ref, 2, start)
        u = keys * values
        put_rows(u_ref, start, u)
        return u

    def absorb(state, u):
        for i in range(8):
            state = decay * state + u[i][None]
        return state

    zero_state = jnp.zeros((MODES, SUB, LANES), F32)

    @pl.loop(1, ROWS // 8)
    def _(b):
        gated(b * 8)

    main_end = lax.fori_loop(1, ROWS // 8, lambda b, state: absorb(state, rows_of(u_ref, b * 8, 8)), zero_state)

    pl.semaphore_wait(barrier, 2 + (ROW_DEVICES - 1) + (X_COUNT - 1) + 7)

    def forward_halo(s):
        return pltpu.make_async_remote_copy(
            src_ref=s_ref.at[s, pl.ds((HALO + ROWS - 6) * SUB, 6 * SUB), :],
            dst_ref=s_ref.at[s, pl.ds((HALO - 6) * SUB, 6 * SUB), :],
            send_sem=halo_send.at[s], recv_sem=halo_recv.at[s],
            device_id={"ctx": next_ctx}, device_id_type=MESH,
        )

    def backward_halo(s):
        if s < 3:
            source = s_ref.at[s, pl.ds(HALO * SUB, EXT * SUB), :]
            target = s_ref.at[s, pl.ds((HALO + ROWS) * SUB, EXT * SUB), :]
        else:
            source = og_ref.at[pl.ds(0, EXT * SUB), :]
            target = og_ref.at[pl.ds(ROWS * SUB, EXT * SUB), :]
        return pltpu.make_async_remote_copy(
            src_ref=source, dst_ref=target, send_sem=halo_send.at[3 + s], recv_sem=halo_recv.at[3 + s],
            device_id={"ctx": prev_ctx}, device_id_type=MESH,
        )

    for s in range(3):
        forward_halo(s).start()
    for s in range(4):
        backward_halo(s).start()

    first_device = ctx == 0
    for s in range(3):
        forward_halo(s).wait_recv()
        halo_rows = s_ref[s, pl.ds((HALO - 6) * SUB, 6 * SUB), :]
        s_ref[s, pl.ds((HALO - 6) * SUB, 6 * SUB), :] = jnp.where(first_device, jnp.zeros_like(halo_rows), halo_rows)
    head_end = absorb(zero_state, gated(0))
    head_decay = jnp.exp(rows_of(rt_ref, 0, MODES) * (-float(ROWS - 8)))
    local_end = main_end + head_decay * head_end

    def halves(target, value):
        for mode in range(MODES):
            target[2 * mode] = value[mode, 0:4]
            target[2 * mode + 1] = value[mode, 4:8]

    def exchange(source, target, send_sem, recv_sem, i):
        peer = lax.rem(place + i, ROW_DEVICES)
        return pltpu.make_async_remote_copy(
            src_ref=source.at[peer], dst_ref=target.at[place], send_sem=send_sem.at[i], recv_sem=recv_sem.at[i],
            device_id={"ctx": row * ROW_DEVICES + peer}, device_id_type=MESH,
        )

    def exchange_start(source, target, send_sem, recv_sem):
        @pl.loop(1, ROW_DEVICES)
        def _(i):
            exchange(source, target, send_sem, recv_sem, i).start()

        target[place] = source[place]

    def exchange_wait(source, target, send_sem, recv_sem):
        @pl.loop(1, ROW_DEVICES)
        def _(i):
            exchange(source, target, send_sem, recv_sem, i).wait()

    def x_copy(source, target, which, i):
        peer = lax.rem(row + i, X_COUNT)
        return pltpu.make_async_remote_copy(
            src_ref=source, dst_ref=target.at[row], send_sem=x_send.at[which, i], recv_sem=x_recv.at[which, i],
            device_id={"ctx": peer * ROW_DEVICES + place}, device_id_type=MESH,
        )

    def reduce_states(erecv, pbuf, rbuf, rrecv, which):
        reverse = which == 1
        own_decay = pow_ref[1]

        def step(i, total):
            j = ROW_DEVICES - 1 - i if reverse else i
            pbuf[j] = total
            return own_decay * total + erecv[j]

        total = lax.fori_loop(0, ROW_DEVICES, step, jnp.zeros((4, LANES), F32))
        rbuf[...] = total
        for i in range(1, X_COUNT):
            x_copy(rbuf, rrecv, which, i).start()
        rrecv[row] = total
        for i in range(1, X_COUNT):
            x_copy(rbuf, rrecv, which, i).wait()
        row_decay = pow_ref[ROW_DEVICES]
        entering = jnp.zeros((4, LANES), F32)
        for i in range(X_COUNT):
            j = X_COUNT - 1 - i if reverse else i
            before = j > row if reverse else j < row
            entering = jnp.where(before, row_decay * entering + rrecv[j], entering)

        @pl.loop(0, ROW_DEVICES)
        def _(i):
            j = ROW_DEVICES - 1 - i if reverse else i
            pbuf[j] = pbuf[j] + pow_ref[i] * entering

    def full_states(source):
        return jnp.stack(
            [jnp.concatenate([source[2 * mode], source[2 * mode + 1]], axis=0) for mode in range(MODES)], axis=0
        )

    halves(ebuf_f, local_end)
    exchange_start(ebuf_f, erecv_f, up_send.at[0], up_recv.at[0])

    scale = rows_of(sc_ref, 0, MODES)

    for s in range(4):
        backward_halo(s).wait_recv()
    gated(ROWS)

    @pl.loop(0, BLOCKS)
    def _(b):
        short(q_ref, 0, b * 8)
        put_rows(sg_ref, b * 8, rows_of(og_ref, b * 8, 8) * gain[None])

    def local_rows(b, state):
        u = rows_of(u_ref, b * 8, 8)
        for i in range(8):
            state = decay * state + u[i][None]
            put_rows(y_ref, b * 8 + i, jnp.sum(scale * state, axis=0, keepdims=True))
        return state

    exchange_wait(ebuf_f, erecv_f, up_send.at[0], up_recv.at[0])
    reduce_states(erecv_f, pbuf_f, rbuf_f, rrecv_f, 0)
    exchange_start(pbuf_f, irecv_f, down_send.at[0], down_recv.at[0])
    lax.fori_loop(0, BLOCKS, local_rows, zero_state)
    part_ref[...] = jnp.zeros_like(part_ref)
    exchange_wait(pbuf_f, irecv_f, down_send.at[0], down_recv.at[0])

    def carried_rows(b, moving):
        local = rows_of(y_ref, b * 8, 8)
        rows = []
        for i in range(8):
            moving = moving * decay
            rows.append(local[i] + jnp.sum(moving, axis=0))
        long_conv = jnp.stack(rows, axis=0)
        put_rows(y_ref, b * 8, long_conv)
        modulated = rows_of(q_ref, b * 8, 8) * long_conv
        put_rows(m_ref, b * 8, modulated)
        part_ref[pl.ds(pl.multiple_of(b * 8, 8), 8), :] = jnp.sum(modulated * modulated, axis=1)
        part_ref[pl.ds(pl.multiple_of(256 + b * 8, 8), 8), :] = jnp.sum(
            modulated * rows_of(sg_ref, b * 8, 8), axis=1
        )
        return moving

    lax.fori_loop(0, BLOCKS, carried_rows, scale * full_states(irecv_f))
    totals = lax.dot_general(
        jnp.ones((SUB, LANES), F32), part_ref[...], (((1,), (1,)), ((), ())), precision=lax.Precision.HIGHEST,
        preferred_element_type=F32,
    )
    for i in range(4):
        sums[i : i + 1, :] = totals[0:1, i * LANES : (i + 1) * LANES]

    def y_copy(i):
        peer = lax.rem(tp + i, 8)
        return pltpu.make_async_remote_copy(
            src_ref=sums, dst_ref=sums_recv.at[tp], send_sem=y_send.at[i], recv_sem=y_recv.at[i],
            device_id={"tp": peer}, device_id_type=MESH,
        )

    for i in range(1, 8):
        y_copy(i).start()
    sums_recv[tp] = sums[...]
    for i in range(1, 8):
        y_copy(i).wait()
    summed = jnp.sum(sums_recv[...], axis=0)
    width = float(8 * TILES * LANES)
    inverse = lax.rsqrt(summed[0:2] / width + EPSILON)
    cross = inverse * inverse * inverse * (summed[2:4] / width)
    last_device = ctx == ctx_count - 1
    for target, value in ((inv_ref, inverse), (cw_ref, cross)):
        target[0:ROWS, :] = jnp.transpose(jnp.broadcast_to(value[0:1, :], (LANES, LANES)))
        tail = jnp.transpose(jnp.broadcast_to(value[1:2, :], (LANES, LANES)))[0:EXT, :]
        target[ROWS : ROWS + EXT, :] = jnp.where(last_device, jnp.zeros_like(tail), tail)

    def mixed_rows(b, state):
        start = b * 8
        grad = rows_of(sg_ref, start, 8)
        modulated = rows_of(m_ref, start, 8)
        inverse_rows = inv_ref[pl.ds(pl.multiple_of(start, 8), 8), :].reshape(8, 1, LANES)
        cross_rows = cw_ref[pl.ds(pl.multiple_of(start, 8), 8), :].reshape(8, 1, LANES)
        mixed = inverse_rows * grad - modulated * cross_rows
        put_rows(qg_ref, start, mixed * rows_of(y_ref, start, 8))
        long_grad = mixed * rows_of(q_ref, start, 8)
        put_rows(lg_ref, start, long_grad)
        for i in range(7, -1, -1):
            state = decay * state + long_grad[i][None]
        return state

    adjoint_end = lax.fori_loop(0, BLOCKS - 1, lambda b, state: mixed_rows(BLOCKS - 1 - b, state), zero_state)
    halves(ebuf_b, adjoint_end)
    exchange_start(ebuf_b, erecv_b, up_send.at[1], up_recv.at[1])

    mixed_rows(0, zero_state)

    def round_rows(source, target, start):
        for tile in range(TILES):
            target[pl.ds(pl.multiple_of(start, 16), 16), tile * LANES : (tile + 1) * LANES] = gathered(
                source, start, 16, tile
            ).astype(BF16)

    @pl.loop(0, ROWS // 8)
    def _(b):
        inverse_rows = inv_ref[pl.ds(pl.multiple_of(b * 8, 8), 8), :].reshape(8, 1, LANES)
        put_rows(m_ref, b * 8, gain[None] * rows_of(m_ref, b * 8, 8) * inverse_rows)

    @pl.loop(0, ROWS // 16)
    def _(b):
        round_rows(m_ref, obuf, b * 16)

    store_output = pltpu.make_async_copy(obuf, output_hbm, out_sem.at[3])
    store_output.start()

    def anticausal(source, s, start):
        window = rows_of(source, start, 8 + TAPS - 1)
        total = rows_of(w_ref.at[s], 0, 1) * window[0:8]
        for tap in range(1, TAPS):
            total = total + rows_of(w_ref.at[s], tap, 1) * window[tap : tap + 8]
        return total

    exchange_wait(ebuf_b, erecv_b, up_send.at[1], up_recv.at[1])
    reduce_states(erecv_b, pbuf_b, rbuf_b, rrecv_b, 1)
    exchange_start(pbuf_b, irecv_b, down_send.at[1], down_recv.at[1])

    @pl.loop(0, ROWS // 8)
    def _(b):
        put_rows(m_ref, b * 8, anticausal(qg_ref, 0, b * 8))

    @pl.loop(0, ROWS // 16)
    def _(b):
        round_rows(m_ref, gbuf.at[0], b * 16)

    def store_grad(s):
        return pltpu.make_async_copy(gbuf.at[s], grads_hbm.at[s], out_sem.at[s])

    store_grad(0).start()

    def local_back(b, state):
        start = (BLOCKS - 1 - b) * 8
        long_grad = rows_of(lg_ref, start, 8)
        for i in range(7, -1, -1):
            state = decay * state + long_grad[i][None]
            put_rows(y_ref, start + i, jnp.sum(scale * state, axis=0, keepdims=True))
        return state

    lax.fori_loop(0, BLOCKS, local_back, zero_state)
    exchange_wait(pbuf_b, irecv_b, down_send.at[1], down_recv.at[1])

    def carried_back(b, moving):
        start = (BLOCKS - 1 - b) * 8
        local = rows_of(y_ref, start, 8)
        rows = [None] * 8
        for i in range(7, -1, -1):
            moving = moving * decay
            rows[i] = local[i] + jnp.sum(moving, axis=0)
        gated_grad = jnp.stack(rows, axis=0)
        put_rows(lg_ref, start, gated_grad * rows_of(v_ref, start, 8))
        put_rows(qg_ref, start, gated_grad * rows_of(k_ref, start, 8))
        return moving

    lax.fori_loop(0, BLOCKS, carried_back, scale * full_states(irecv_b))
    for s, source, target in ((1, lg_ref, y_ref), (2, qg_ref, m_ref)):

        @pl.loop(0, ROWS // 8)
        def _(b):
            put_rows(target, b * 8, anticausal(source, s, b * 8))

        @pl.loop(0, ROWS // 16)
        def _(b):
            round_rows(target, gbuf.at[s], b * 16)

        store_grad(s).start()
    for s in range(3):
        forward_halo(s).wait_send()
    for s in range(4):
        backward_halo(s).wait_send()
    store_output.wait()
    for s in range(3):
        store_grad(s).wait()


def on_device(streams, short_filter, decay_rate, residue, norm_gain, out_grad):
    positions = ROWS + EXT
    tiles = lambda count: pltpu.VMEM((count * SUB, LANES), F32)
    states = lambda: [
        pltpu.VMEM((ROW_DEVICES, 4, LANES), F32),
        pltpu.VMEM((ROW_DEVICES, 4, LANES), F32),
        pltpu.VMEM((ROW_DEVICES, 4, LANES), F32),
        pltpu.VMEM((ROW_DEVICES, 4, LANES), F32),
        pltpu.VMEM((4, LANES), F32),
        pltpu.VMEM((X_COUNT, 4, LANES), F32),
    ]
    scratch = [
        pltpu.VMEM(streams.shape, BF16),
        pltpu.VMEM(out_grad.shape, BF16),
        pltpu.VMEM(out_grad.shape, BF16),
        pltpu.VMEM(streams.shape, BF16),
        pltpu.VMEM((3, (HALO + positions) * SUB, LANES), F32),
        pltpu.VMEM((3, 8 * SUB, LANES), F32),
        tiles(MODES),
        tiles(MODES),
        tiles(MODES),
        *[tiles(positions) for _ in range(10)],
        pltpu.VMEM((512, LANES), F32),
        pltpu.VMEM((positions, LANES), F32),
        pltpu.VMEM((positions, LANES), F32),
        pltpu.VMEM((ROW_DEVICES, 4, LANES), F32),
        pltpu.VMEM((ROW_DEVICES + 1, 4, LANES), F32),
        *states(),
        *states(),
        pltpu.VMEM((4, LANES), F32),
        pltpu.VMEM((8, 4, LANES), F32),
        pltpu.SemaphoreType.DMA((2,)),
        pltpu.SemaphoreType.DMA((4,)),
        pltpu.SemaphoreType.DMA((7,)),
        pltpu.SemaphoreType.DMA((7,)),
        pltpu.SemaphoreType.DMA((2, ROW_DEVICES)),
        pltpu.SemaphoreType.DMA((2, ROW_DEVICES)),
        pltpu.SemaphoreType.DMA((2, ROW_DEVICES)),
        pltpu.SemaphoreType.DMA((2, ROW_DEVICES)),
        pltpu.SemaphoreType.DMA((2, X_COUNT)),
        pltpu.SemaphoreType.DMA((2, X_COUNT)),
        pltpu.SemaphoreType.DMA((8,)),
        pltpu.SemaphoreType.DMA((8,)),
    ]
    vmem = pl.BlockSpec(memory_space=pltpu.VMEM)
    anywhere = pl.BlockSpec(memory_space=pl.ANY)
    taps = jnp.pad(jnp.transpose(short_filter, (0, 2, 1)), ((0, 0), (0, 1), (0, 0)))
    return pl.pallas_call(
        kernel,
        out_shape=(
            jax.ShapeDtypeStruct(out_grad.shape, BF16),
            jax.ShapeDtypeStruct(streams.shape, BF16),
        ),
        in_specs=[anywhere, vmem, vmem, vmem, vmem, anywhere],
        out_specs=(anywhere, anywhere),
        scratch_shapes=scratch,
        compiler_params=pltpu.CompilerParams(collective_id=0, has_side_effects=True, vmem_limit_bytes=48 * 2**20),
        name="hyena",
    )(streams, taps, decay_rate, residue, norm_gain.reshape(SUB, LANES), out_grad)


def solution(mesh):
    return jax.shard_map(
        on_device,
        mesh=mesh,
        in_specs=(
            P(None, "ctx", "tp"),
            P(None, "tp", None),
            P(None, "tp"),
            P(None, "tp"),
            P("tp"),
            P("ctx", "tp"),
        ),
        out_specs=(P("ctx", "tp"), P(None, "ctx", "tp")),
        check_vma=False,
    )
```

```python
import functools

import jax
import jax.numpy as jnp
from jax import lax
from jax.experimental import pallas as pl
from jax.experimental.pallas import tpu as pltpu
from jax.sharding import PartitionSpec as P

MESH = pl.DeviceIdType.MESH
F32 = jnp.float32
BF16 = jnp.bfloat16
GROUP = 16
EPSILON = 1e-05
ROWS = 128
EXT = 8
HALO = 8
TAPS = 7
MODES = 16
SUB = 8
LANES = 128
TILES = 8
ROW_DEVICES = 32
X_COUNT = 4
BLOCKS = (ROWS + EXT) // 8
VMEM_LIMIT = 62 * 2**20


def rows_of(ref, start, count):
    offset = start * SUB
    if not isinstance(offset, int):
        offset = pl.multiple_of(offset, SUB)
    return ref[pl.ds(offset, count * SUB), :].reshape(count, SUB, LANES)


def put_rows(ref, start, value):
    offset = start * SUB
    if not isinstance(offset, int):
        offset = pl.multiple_of(offset, SUB)
    ref[pl.ds(offset, value.shape[0] * SUB), :] = value.reshape(value.shape[0] * SUB, LANES)


def spread(ref, start, tile, value):
    ref[pl.ds(start * SUB + tile, value.shape[0], stride=SUB), :] = value


def gathered(ref, start, count, tile):
    return ref[pl.ds(start * SUB + tile, count, stride=SUB), :]


def kernel(
    streams_hbm, filter_hbm, rate_hbm, residue_hbm, gain_hbm, grad_hbm,
    obuf, gbuf,
    filter_ref, rate_ref, residue_ref, gain_ref, xin, gin, s_ref, w_ref, r_ref, sc_ref, rt_ref, q_ref, k_ref, v_ref, u_ref, og_ref, sg_ref, y_ref, m_ref,
    lg_ref, qg_ref, part_ref, inv_ref, cw_ref, rate4, pow_ref, back_ref,
    ebuf_f, erecv_f, pbuf_f, irecv_f, rbuf_f, rrecv_f,
    ebuf_b, erecv_b, pbuf_b, irecv_b, rbuf_b, rrecv_b,
    sums, sums_recv,
    in_sem, halo_send, halo_recv, up_send, up_recv, down_send, down_recv, x_send, x_recv, y_send, y_recv,
):
    ctx = lax.axis_index("ctx")
    tp = lax.axis_index("tp")
    place = lax.rem(ctx, ROW_DEVICES)
    row = lax.div(ctx, ROW_DEVICES)
    ctx_count = ROW_DEVICES * X_COUNT
    next_ctx = lax.rem(ctx + 1, ctx_count)
    prev_ctx = lax.rem(ctx + ctx_count - 1, ctx_count)

    loads = [
        pltpu.make_async_copy(source, target, in_sem.at[i])
        for i, (source, target) in enumerate(
            (
                (rate_hbm, rate_ref),
                (filter_hbm, filter_ref),
                (streams_hbm.at[1], xin.at[1]),
                (streams_hbm.at[2], xin.at[2]),
                (residue_hbm, residue_ref),
                (streams_hbm.at[0], xin.at[0]),
                (grad_hbm, gin),
                (gain_hbm, gain_ref),
            )
        )
    ]
    for load in loads:
        load.start()

    def far_first(visit):
        visit(ROW_DEVICES // 2)

        @pl.loop(1, ROW_DEVICES // 2)
        def _(i):
            visit(ROW_DEVICES // 2 - i)
            visit(ROW_DEVICES // 2 + i)

    barrier = pltpu.get_barrier_semaphore()

    def greet_ctx(peer):
        pl.semaphore_signal(barrier, inc=1, device_id={"ctx": peer}, device_id_type=MESH)

    far_first(lambda i: greet_ctx(row * ROW_DEVICES + lax.rem(place + i, ROW_DEVICES)))
    for i in (4, 3, 5, 2, 6, 1, 7):
        pl.semaphore_signal(barrier, inc=1, device_id={"tp": lax.rem(tp + i, 8)}, device_id_type=MESH)
    for i in (2, 1, 3):
        greet_ctx(lax.rem(row + i, X_COUNT) * ROW_DEVICES + place)
    greet_ctx(next_ctx)
    greet_ctx(prev_ctx)

    loads[0].wait()
    for half in range(2):
        for tile in range(TILES):
            lanes = slice(tile * LANES, (tile + 1) * LANES)
            rate = rate_ref[half * 8 : half * 8 + 8, lanes]
            spread(rt_ref, half * 8, tile, rate)
            spread(r_ref, half * 8, tile, jnp.exp(-rate))
    loads[1].wait()
    groups = filter_ref.shape[2]
    spreader = (
        lax.broadcasted_iota(jnp.int32, (groups, TILES * LANES), 1) // GROUP
        == lax.broadcasted_iota(jnp.int32, (groups, TILES * LANES), 0)
    ).astype(F32)
    for s in range(3):
        taps = lax.dot_general(
            filter_ref[s].astype(F32), spreader, (((1,), (0,)), ((), ())), precision=lax.Precision.HIGHEST,
            preferred_element_type=F32,
        )
        for tile in range(TILES):
            spread(w_ref.at[s], 0, tile, taps[:, tile * LANES : (tile + 1) * LANES])
    decay = rows_of(r_ref, 0, MODES)

    def to_tiles(s):
        @pl.loop(0, ROWS // 16)
        def _(b):
            for tile in range(TILES):
                value = xin[s, pl.ds(b * 16, 16), tile * LANES : (tile + 1) * LANES].astype(F32)
                spread(s_ref.at[s], HALO + b * 16, tile, value)

    loads[2].wait()
    to_tiles(1)
    loads[3].wait()
    to_tiles(2)

    def short(target, s, start):
        window = rows_of(s_ref.at[s], start + HALO - (TAPS - 1), 8 + TAPS - 1)
        total = rows_of(w_ref.at[s], 0, 1) * window[TAPS - 1 : TAPS - 1 + 8]
        for tap in range(1, TAPS):
            total = total + rows_of(w_ref.at[s], tap, 1) * window[TAPS - 1 - tap : TAPS - 1 - tap + 8]
        if target is not None:
            put_rows(target, start, total)
        return total

    def gated(start):
        keys = short(k_ref, 1, start)
        values = short(v_ref, 2, start)
        u = keys * values
        put_rows(u_ref, start, u)
        return u

    def absorb(state, u):
        for i in range(8):
            state = decay * state + u[i][None]
        return state

    zero_state = jnp.zeros((MODES, SUB, LANES), F32)

    @pl.loop(1, ROWS // 8)
    def _(b):
        gated(b * 8)

    main_end = lax.fori_loop(1, ROWS // 8, lambda b, state: absorb(state, rows_of(u_ref, b * 8, 8)), zero_state)

    pl.semaphore_wait(barrier, 2 + (ROW_DEVICES - 1) + (X_COUNT - 1) + 7)

    def forward_halo(s):
        return pltpu.make_async_remote_copy(
            src_ref=s_ref.at[s, pl.ds((HALO + ROWS - 6) * SUB, 6 * SUB), :],
            dst_ref=s_ref.at[s, pl.ds((HALO - 6) * SUB, 6 * SUB), :],
            send_sem=halo_send.at[s], recv_sem=halo_recv.at[s],
            device_id={"ctx": next_ctx}, device_id_type=MESH,
        )

    def backward_halo(s):
        if s < 3:
            source = s_ref.at[s, pl.ds(HALO * SUB, EXT * SUB), :]
            target = s_ref.at[s, pl.ds((HALO + ROWS) * SUB, EXT * SUB), :]
        else:
            source = og_ref.at[pl.ds(0, EXT * SUB), :]
            target = og_ref.at[pl.ds(ROWS * SUB, EXT * SUB), :]
        return pltpu.make_async_remote_copy(
            src_ref=source, dst_ref=target, send_sem=halo_send.at[3 + s], recv_sem=halo_recv.at[3 + s],
            device_id={"ctx": prev_ctx}, device_id_type=MESH,
        )

    for s in (1, 2):
        forward_halo(s).start()
    head_decay = jnp.exp(rows_of(rt_ref, 0, MODES) * (-float(ROWS - 8)))
    first_device = ctx == 0

    def receive_head(s):
        forward_halo(s).wait_recv()
        halo_rows = s_ref[s, pl.ds((HALO - 6) * SUB, 6 * SUB), :]
        s_ref[s, pl.ds((HALO - 6) * SUB, 6 * SUB), :] = jnp.where(first_device, jnp.zeros_like(halo_rows), halo_rows)

    for s in (1, 2):
        receive_head(s)
    head_end = absorb(zero_state, gated(0))
    local_end = main_end + head_decay * head_end

    def halves(target, value):
        for mode in range(MODES):
            target[2 * mode] = value[mode, 0:4]
            target[2 * mode + 1] = value[mode, 4:8]

    def exchange(source, target, send_sem, recv_sem, i):
        peer = lax.rem(place + i, ROW_DEVICES)
        return pltpu.make_async_remote_copy(
            src_ref=source.at[peer], dst_ref=target.at[place], send_sem=send_sem.at[i], recv_sem=recv_sem.at[i],
            device_id={"ctx": row * ROW_DEVICES + peer}, device_id_type=MESH,
        )

    def exchange_start(source, target, send_sem, recv_sem):
        far_first(lambda i: exchange(source, target, send_sem, recv_sem, i).start())
        target[place] = source[place]

    def exchange_wait(source, target, send_sem, recv_sem, arrived=None):
        def one(i, total):
            exchange(source, target, send_sem, recv_sem, i).wait()
            return total if arrived is None else arrived(lax.rem(place - i + ROW_DEVICES, ROW_DEVICES), total)

        total = jnp.zeros((4, LANES), F32) if arrived is None else arrived(place, None)
        total = lax.fori_loop(
            1, ROW_DEVICES // 2, lambda i, total: one(ROW_DEVICES - i, one(i, total)), total
        )
        return one(ROW_DEVICES // 2, total)

    def x_copy(source, target, which, i):
        peer = lax.rem(row + i, X_COUNT)
        return pltpu.make_async_remote_copy(
            src_ref=source, dst_ref=target.at[row], send_sem=x_send.at[which, i], recv_sem=x_recv.at[which, i],
            device_id={"ctx": peer * ROW_DEVICES + place}, device_id_type=MESH,
        )

    def reduce_states(ebuf, erecv, pbuf, rbuf, rrecv, which):
        reverse = which == 1
        own_decay = pow_ref[1]
        reach = pow_ref if reverse else back_ref

        def arrived(j, total):
            term = reach[j] * erecv[j]
            return term if total is None else total + term

        total = exchange_wait(ebuf, erecv, up_send.at[which], up_recv.at[which], arrived)
        rbuf[...] = total
        rrecv[row] = total
        for i in (2, 1, 3):
            x_copy(rbuf, rrecv, which, i).start()
        ahead = jnp.zeros((4, LANES), F32)
        for i in range(ROW_DEVICES):
            j = ROW_DEVICES - 1 - i if reverse else i
            pbuf[j] = ahead
            ahead = own_decay * ahead + erecv[j]
        for i in (1, 3, 2):
            x_copy(rbuf, rrecv, which, i).wait()
        row_decay = pow_ref[ROW_DEVICES]
        entering = jnp.zeros((4, LANES), F32)
        for i in range(X_COUNT):
            j = X_COUNT - 1 - i if reverse else i
            before = j > row if reverse else j < row
            entering = jnp.where(before, row_decay * entering + rrecv[j], entering)
        powers = back_ref[...] if reverse else pow_ref[0:ROW_DEVICES]
        pbuf[...] = pbuf[...] + powers * entering[None]

    def full_states(source):
        return jnp.stack(
            [jnp.concatenate([source[2 * mode], source[2 * mode + 1]], axis=0) for mode in range(MODES)], axis=0
        )

    halves(ebuf_f, local_end)
    exchange_start(ebuf_f, erecv_f, up_send.at[0], up_recv.at[0])

    loads[5].wait()
    to_tiles(0)
    forward_halo(0).start()
    loads[6].wait()

    @pl.loop(0, ROWS // 16)
    def _(b):
        for tile in range(TILES):
            value = gin[pl.ds(b * 16, 16), tile * LANES : (tile + 1) * LANES].astype(F32)
            spread(og_ref, b * 16, tile, value)

    for s in range(4):
        backward_halo(s).start()
    loads[4].wait()
    for half in range(2):
        for tile in range(TILES):
            lanes = slice(tile * LANES, (tile + 1) * LANES)
            residue = residue_ref[half * 8 : half * 8 + 8, lanes]
            rate = rate_ref[half * 8 : half * 8 + 8, lanes]
            spread(sc_ref, half * 8, tile, residue * jnp.sqrt(2.0 * rate))
    for mode in range(MODES):
        rates = rt_ref[mode * SUB : mode * SUB + SUB, :]
        rate4[2 * mode] = rates[0:4]
        rate4[2 * mode + 1] = rates[4:8]
    own_rate = rate4[place] * float(ROWS)

    @pl.loop(0, ROW_DEVICES + 1)
    def _(i):
        pow_ref[i] = jnp.exp(-own_rate * i.astype(F32))

    @pl.loop(0, ROW_DEVICES)
    def _(i):
        back_ref[i] = pow_ref[ROW_DEVICES - 1 - i]

    loads[7].wait()
    gain = gain_ref[...]
    scale = rows_of(sc_ref, 0, MODES)
    receive_head(0)
    for s in range(4):
        backward_halo(s).wait_recv()
    gated(ROWS)

    @pl.loop(0, BLOCKS)
    def _(b):
        short(q_ref, 0, b * 8)
        put_rows(sg_ref, b * 8, rows_of(og_ref, b * 8, 8) * gain[None])

    def local_rows(b, state):
        u = rows_of(u_ref, b * 8, 8)
        for i in range(8):
            state = decay * state + u[i][None]
            put_rows(y_ref, b * 8 + i, jnp.sum(scale * state, axis=0, keepdims=True))
        return state

    reduce_states(ebuf_f, erecv_f, pbuf_f, rbuf_f, rrecv_f, 0)
    exchange_start(pbuf_f, irecv_f, down_send.at[0], down_recv.at[0])
    lax.fori_loop(0, BLOCKS, local_rows, zero_state)
    part_ref[...] = jnp.zeros_like(part_ref)
    exchange_wait(pbuf_f, irecv_f, down_send.at[0], down_recv.at[0])

    def carried_rows(b, moving):
        local = rows_of(y_ref, b * 8, 8)
        rows = []
        for i in range(8):
            moving = moving * decay
            rows.append(local[i] + jnp.sum(moving, axis=0))
        long_conv = jnp.stack(rows, axis=0)
        put_rows(y_ref, b * 8, long_conv)
        modulated = rows_of(q_ref, b * 8, 8) * long_conv
        put_rows(m_ref, b * 8, modulated)
        part_ref[pl.ds(pl.multiple_of(b * 8, 8), 8), :] = jnp.sum(modulated * modulated, axis=1)
        part_ref[pl.ds(pl.multiple_of(256 + b * 8, 8), 8), :] = jnp.sum(
            modulated * rows_of(sg_ref, b * 8, 8), axis=1
        )
        return moving

    lax.fori_loop(0, BLOCKS, carried_rows, scale * full_states(irecv_f))
    totals = lax.dot_general(
        jnp.ones((SUB, LANES), F32), part_ref[...], (((1,), (1,)), ((), ())), precision=lax.Precision.HIGHEST,
        preferred_element_type=F32,
    )
    for i in range(4):
        sums[i : i + 1, :] = totals[0:1, i * LANES : (i + 1) * LANES]

    def y_copy(i):
        peer = lax.rem(tp + i, 8)
        return pltpu.make_async_remote_copy(
            src_ref=sums, dst_ref=sums_recv.at[tp], send_sem=y_send.at[i], recv_sem=y_recv.at[i],
            device_id={"tp": peer}, device_id_type=MESH,
        )

    for i in (4, 3, 5, 2, 6, 1, 7):
        y_copy(i).start()
    sums_recv[tp] = sums[...]
    for i in (1, 7, 2, 6, 3, 5, 4):
        y_copy(i).wait()
    summed = jnp.sum(sums_recv[...], axis=0)
    width = float(8 * TILES * LANES)
    inverse = lax.rsqrt(summed[0:2] / width + EPSILON)
    cross = inverse * inverse * inverse * (summed[2:4] / width)
    last_device = ctx == ctx_count - 1
    for target, value in ((inv_ref, inverse), (cw_ref, cross)):
        target[0:ROWS, :] = jnp.transpose(jnp.broadcast_to(value[0:1, :], (LANES, LANES)))
        tail = jnp.transpose(jnp.broadcast_to(value[1:2, :], (LANES, LANES)))[0:EXT, :]
        target[ROWS : ROWS + EXT, :] = jnp.where(last_device, jnp.zeros_like(tail), tail)

    def mixed_rows(b, state):
        start = b * 8
        grad = rows_of(sg_ref, start, 8)
        modulated = rows_of(m_ref, start, 8)
        inverse_rows = inv_ref[pl.ds(pl.multiple_of(start, 8), 8), :].reshape(8, 1, LANES)
        cross_rows = cw_ref[pl.ds(pl.multiple_of(start, 8), 8), :].reshape(8, 1, LANES)
        mixed = inverse_rows * grad - modulated * cross_rows
        put_rows(qg_ref, start, mixed * rows_of(y_ref, start, 8))
        long_grad = mixed * rows_of(q_ref, start, 8)
        put_rows(lg_ref, start, long_grad)
        for i in range(7, -1, -1):
            state = decay * state + long_grad[i][None]
        return state

    adjoint_end = lax.fori_loop(0, BLOCKS - 1, lambda b, state: mixed_rows(BLOCKS - 1 - b, state), zero_state)
    halves(ebuf_b, adjoint_end)
    exchange_start(ebuf_b, erecv_b, up_send.at[1], up_recv.at[1])

    mixed_rows(0, zero_state)

    def round_rows(source, target, start):
        for tile in range(TILES):
            target[pl.ds(pl.multiple_of(start, 16), 16), tile * LANES : (tile + 1) * LANES] = gathered(
                source, start, 16, tile
            ).astype(BF16)

    @pl.loop(0, ROWS // 8)
    def _(b):
        inverse_rows = inv_ref[pl.ds(pl.multiple_of(b * 8, 8), 8), :].reshape(8, 1, LANES)
        put_rows(m_ref, b * 8, gain[None] * rows_of(m_ref, b * 8, 8) * inverse_rows)

    @pl.loop(0, ROWS // 16)
    def _(b):
        round_rows(m_ref, obuf, b * 16)

    def anticausal(source, s, start):
        window = rows_of(source, start, 8 + TAPS - 1)
        total = rows_of(w_ref.at[s], 0, 1) * window[0:8]
        for tap in range(1, TAPS):
            total = total + rows_of(w_ref.at[s], tap, 1) * window[tap : tap + 8]
        return total

    reduce_states(ebuf_b, erecv_b, pbuf_b, rbuf_b, rrecv_b, 1)
    exchange_start(pbuf_b, irecv_b, down_send.at[1], down_recv.at[1])

    @pl.loop(0, ROWS // 8)
    def _(b):
        put_rows(m_ref, b * 8, anticausal(qg_ref, 0, b * 8))

    @pl.loop(0, ROWS // 16)
    def _(b):
        round_rows(m_ref, gbuf.at[0], b * 16)

    def local_back(b, state):
        start = (BLOCKS - 1 - b) * 8
        long_grad = rows_of(lg_ref, start, 8)
        for i in range(7, -1, -1):
            state = decay * state + long_grad[i][None]
            put_rows(y_ref, start + i, jnp.sum(scale * state, axis=0, keepdims=True))
        return state

    lax.fori_loop(0, BLOCKS, local_back, zero_state)
    exchange_wait(pbuf_b, irecv_b, down_send.at[1], down_recv.at[1])

    def carried_back(b, moving):
        start = (BLOCKS - 1 - b) * 8
        local = rows_of(y_ref, start, 8)
        rows = [None] * 8
        for i in range(7, -1, -1):
            moving = moving * decay
            rows[i] = local[i] + jnp.sum(moving, axis=0)
        gated_grad = jnp.stack(rows, axis=0)
        put_rows(lg_ref, start, gated_grad * rows_of(v_ref, start, 8))
        put_rows(qg_ref, start, gated_grad * rows_of(k_ref, start, 8))
        return moving

    lax.fori_loop(0, BLOCKS, carried_back, scale * full_states(irecv_b))
    for s, source, target in ((1, lg_ref, y_ref), (2, qg_ref, m_ref)):

        @pl.loop(0, ROWS // 8)
        def _(b):
            put_rows(target, b * 8, anticausal(source, s, b * 8))

        @pl.loop(0, ROWS // 16)
        def _(b):
            round_rows(target, gbuf.at[s], b * 16)

    for s in range(3):
        forward_halo(s).wait_send()
    for s in range(4):
        backward_halo(s).wait_send()


def hand_out(output_ref, grads_ref, output_hbm, grads_hbm, sem):
    copies = [pltpu.make_async_copy(grads_ref.at[s], grads_hbm.at[s], sem.at[s]) for s in range(3)]
    copies.append(pltpu.make_async_copy(output_ref, output_hbm, sem.at[3]))
    for copy in copies:
        copy.start()
    for copy in copies:
        copy.wait()


def on_device(streams, short_filter, decay_rate, residue, norm_gain, out_grad):
    positions = ROWS + EXT
    tiles = lambda count: pltpu.VMEM((count * SUB, LANES), F32)
    states = lambda: [
        pltpu.VMEM((ROW_DEVICES, 4, LANES), F32),
        pltpu.VMEM((ROW_DEVICES, 4, LANES), F32),
        pltpu.VMEM((ROW_DEVICES, 4, LANES), F32),
        pltpu.VMEM((ROW_DEVICES, 4, LANES), F32),
        pltpu.VMEM((4, LANES), F32),
        pltpu.VMEM((X_COUNT, 4, LANES), F32),
    ]
    scratch = [
        pltpu.VMEM((3, TAPS, short_filter.shape[1]), BF16),
        pltpu.VMEM(decay_rate.shape, F32),
        pltpu.VMEM(residue.shape, F32),
        pltpu.VMEM((SUB, LANES), F32),
        pltpu.VMEM(streams.shape, BF16),
        pltpu.VMEM(out_grad.shape, BF16),
        pltpu.VMEM((3, (HALO + positions) * SUB, LANES), F32),
        pltpu.VMEM((3, 8 * SUB, LANES), F32),
        tiles(MODES),
        tiles(MODES),
        tiles(MODES),
        *[tiles(positions) for _ in range(10)],
        pltpu.VMEM((512, LANES), F32),
        pltpu.VMEM((positions, LANES), F32),
        pltpu.VMEM((positions, LANES), F32),
        pltpu.VMEM((ROW_DEVICES, 4, LANES), F32),
        pltpu.VMEM((ROW_DEVICES + 1, 4, LANES), F32),
        pltpu.VMEM((ROW_DEVICES, 4, LANES), F32),
        *states(),
        *states(),
        pltpu.VMEM((4, LANES), F32),
        pltpu.VMEM((8, 4, LANES), F32),
        pltpu.SemaphoreType.DMA((8,)),
        pltpu.SemaphoreType.DMA((7,)),
        pltpu.SemaphoreType.DMA((7,)),
        pltpu.SemaphoreType.DMA((2, ROW_DEVICES)),
        pltpu.SemaphoreType.DMA((2, ROW_DEVICES)),
        pltpu.SemaphoreType.DMA((2, ROW_DEVICES)),
        pltpu.SemaphoreType.DMA((2, ROW_DEVICES)),
        pltpu.SemaphoreType.DMA((2, X_COUNT)),
        pltpu.SemaphoreType.DMA((2, X_COUNT)),
        pltpu.SemaphoreType.DMA((8,)),
        pltpu.SemaphoreType.DMA((8,)),
    ]
    stay = pl.BlockSpec(memory_space=pltpu.HBM)
    anywhere = pl.BlockSpec(memory_space=pl.ANY)
    taps = jnp.transpose(short_filter, (0, 2, 1))
    shapes = (jax.ShapeDtypeStruct(out_grad.shape, BF16), jax.ShapeDtypeStruct(streams.shape, BF16))
    output, grads = pl.pallas_call(
        kernel,
        out_shape=tuple(pltpu.VMEM(shape.shape, BF16) for shape in shapes),
        in_specs=[stay] * 6,
        out_specs=(pl.BlockSpec(memory_space=pltpu.VMEM),) * 2,
        scratch_shapes=scratch,
        compiler_params=pltpu.CompilerParams(collective_id=0, has_side_effects=True, vmem_limit_bytes=VMEM_LIMIT),
        name="hyena",
    )(streams, taps, decay_rate, residue, norm_gain.reshape(SUB, LANES), out_grad)
    return pl.pallas_call(
        hand_out,
        out_shape=shapes,
        in_specs=[anywhere] * 2,
        out_specs=(anywhere, anywhere),
        scratch_shapes=[pltpu.SemaphoreType.DMA((4,))],
        compiler_params=pltpu.CompilerParams(vmem_limit_bytes=2**20),
        name="hand_out",
    )(output, grads)


def solution(mesh):
    return jax.shard_map(
        on_device,
        mesh=mesh,
        in_specs=(
            P(None, "ctx", "tp"),
            P(None, "tp", None),
            P(None, "tp"),
            P(None, "tp"),
            P("tp"),
            P("ctx", "tp"),
        ),
        out_specs=(P("ctx", "tp"), P(None, "ctx", "tp")),
        check_vma=False,
    )
```
